32 devices in a mesh: dp: 16 (over z, y, x), tensor: 2 (over core).
Axes of the slice: x: 2, y: 2, z: 4, core: 2. Of those that a mesh axis runs over, the one named last changes fastest.
Arguments:
- tokens: bfloat16 [2, 16, 256, 768], P(None, 'dp', 'tensor'), may hold values from -6 to 6
- lengths: int32 [2, 16, 8], P(None, 'dp'), may hold values from 1 to 64, 256 in all within a row
- qkv_weight: bfloat16 [2, 3, 768, 768], P(None, None, 'dp', 'tensor'), may hold values from -0.21875 to 0.21875
- qkv_bias: bfloat16 [2, 2, 2, 384], P(None, None, 'tensor', 'dp'), may hold values from -3 to 3
- out_weight: bfloat16 [2, 768, 768], P(None, 'tensor', 'dp'), may hold values from -0.875 to 0.875
- up_weight: bfloat16 [2, 768, 3072], P(None, 'dp', 'tensor'), may hold values from -0.21875 to 0.21875
- up_bias: bfloat16 [2, 2, 1536], P(None, 'tensor', 'dp'), may hold values from -3 to 3
- down_weight: bfloat16 [2, 3072, 768], P(None, 'tensor', 'dp'), may hold values from -0.109375 to 0.109375
- norm_gains: bfloat16 [2, 2, 768], P(None, None, 'dp'), may hold values from 0.5 to 1.5
- shifts: bfloat16 [2, 4, 768], P(None, None, 'dp'), may hold values from -2 to 2
- cotangent: bfloat16 [2, 16, 256, 768], P(None, 'dp', 'tensor'), may hold values from -6 to 6
Outputs:
- out_tokens: float32 [2, 16, 256, 768], P(None, 'dp', 'tensor')
- token_grad: float32 [2, 16, 256, 768], P(None, 'dp', 'tensor')
- qkv_weight_grad: float32 [2, 3, 768, 768], P(None, None, 'dp', 'tensor')
- qkv_bias_grad: float32 [2, 2, 2, 384], P(None, None, 'tensor', 'dp')
- out_weight_grad: float32 [2, 768, 768], P(None, 'tensor', 'dp')
- up_weight_grad: float32 [2, 768, 3072], P(None, 'dp', 'tensor')
- up_bias_grad: float32 [2, 2, 1536], P(None, 'tensor', 'dp')
- down_weight_grad: float32 [2, 3072, 768], P(None, 'tensor', 'dp')
- gain_grad: float32 [2, 2, 768], P(None, None, 'dp')
- shift_grad: float32 [2, 4, 768], P(None, None, 'dp')
The draws below stay inside these ranges and needn't reach their ends.
Inputs may be any that keep to these rules, and one draw needn't show every extreme that they name: The 8 lengths of a row sum to 256; in every row the longest is exactly 64.
All inputs are finite; a program needn't handle non-finite values.
Results may differ from the reference program's by a relative error of at most 0.025.
Values may be sent and summed in bfloat16 or wider, within the bound.
No kernel may reach another device: no remote copies, remote signals or barrier semaphores. Data moves between devices by JAX's collectives and lax.ppermute only.
A program may use at most 192 MiB of HBM per device.

```python
import math
import jax
import jax.numpy as jnp
import numpy as np
from jax import lax

D = 768
H = 12
HD = 64
FF = 3072
LEN = 256
DOCS = 8
MICRO = 2
LAYERS = 2
ROWS = 16
MOST = 64
N_TENSOR = 2


def spiked(drawn, rng, source, target, parts, factor):
    owner, partner = [(jnp.arange(drawn.shape[dim]) // (drawn.shape[dim] // parts)).reshape([-1 if axis == dim else 1 for axis in range(drawn.ndim)]) for dim in (source, target)]
    chosen = jax.random.permutation(rng, parts)[partner]
    strong = (owner == chosen) | (owner == (partner + parts // 2) % parts)
    return jnp.where(strong, factor * drawn, drawn)


def shard_levels(own_key, extent, pieces, low, largest):
    loudness, own = 1.0, jax.random.fold_in(own_key, 6)
    for position, shards_of in pieces:
        heights = jnp.exp(jax.random.uniform(jax.random.fold_in(own, position), (shards_of,), jnp.float32, low / len(pieces), largest / len(pieces)))
        loudness = loudness * jnp.repeat(heights, extent[position] // shards_of).reshape([-1 if axis == position else 1 for axis in range(len(extent))])
    return loudness


def profile(amount, total, limit, lean):
    portions = [(1 << 20) // math.isqrt(standing ** lean) + 1 for standing in range(2, amount + 1)]
    surplus, holding = total - limit - (amount - 1), [1] * (amount - 1)
    while surplus > 0:
        free = [i for i in range(amount - 1) if holding[i] < limit]
        pool, left = sum([portions[i] for i in free]), surplus
        for i in free:
            extra = min(limit - holding[i], max(1, left * portions[i] // pool), surplus)
            holding[i] = holding[i] + extra
            surplus = surplus - extra
    return np.array([limit] + holding)


def uneven(key, count, total, reach, skew):
    if count == 2:
        one = jax.random.randint(key, (), max(1, total - reach), min(reach, total - 1) + 1)
        return jnp.stack([one, total - one])
    sizes = jnp.asarray(profile(count, total, reach, skew), jnp.int32)
    couples = (count - 1) // 2
    source_of, taker = sizes[1:1 + 2 * couples:2], sizes[2:2 + 2 * couples:2]
    margin = jnp.minimum(source_of - 1, reach - taker)
    passed = jax.random.randint(jax.random.fold_in(key, 1), (couples,), 0, 1 << 20) % (margin + 1)
    sizes = sizes.at[1:1 + 2 * couples:2].set(source_of - passed).at[2:2 + 2 * couples:2].set(taker + passed)
    return sizes[jax.random.permutation(jax.random.fold_in(key, 2), count)]


def noise(key, shape, scale, reach, split=(), kind=jnp.bfloat16):
    values = scale * jax.random.normal(key, shape, jnp.float32)
    if split:
        values = values * shard_levels(key, shape, split, -0.22, 0.18)
    return jnp.clip(values, -reach, reach).astype(kind)


def heavy_noise(stream_key, extent, scale, limit, split, heavy, held_as=jnp.bfloat16):
    values = scale * jax.random.normal(stream_key, extent, jnp.float32)
    if split:
        values = values * shard_levels(stream_key, extent, split, -0.22, 0.18)
    return jnp.clip(spiked(values, jax.random.fold_in(stream_key, 3), *heavy), -limit, limit).astype(held_as)


def setup_inputs(seed: int = 0) -> dict:
    splits = jax.random.split(jax.random.key(seed), 12)
    return {
        "tokens": noise(splits[0], (MICRO, ROWS, LEN, D), 1.0, 6.0, ((1, 16), (2, 2))),
        "lengths": jax.vmap(lambda own: uneven(own, DOCS, LEN, MOST, 2))(jax.random.split(splits[1], MICRO * ROWS)).reshape((MICRO, ROWS, DOCS)).astype(jnp.int32),
        "qkv_weight": noise(splits[2], (LAYERS, 3, D, D), D ** -0.5, 0.21875, ((2, 16), (3, 2))),
        "qkv_bias": noise(splits[3], (LAYERS, 2, N_TENSOR, D // N_TENSOR), 0.5, 3.0, ((2, 2), (3, 16))),
        "out_weight": noise(splits[4], (LAYERS, D, D), (D // 16) ** -0.5, 0.875, ((1, 2), (2, 16))),
        "up_weight": noise(splits[5], (LAYERS, D, FF), D ** -0.5, 0.21875, ((1, 16), (2, 2))),
        "up_bias": noise(splits[6], (LAYERS, N_TENSOR, FF // N_TENSOR), 0.5, 3.0, ((1, 2), (2, 16))),
        "down_weight": noise(splits[7], (LAYERS, FF, D), FF ** -0.5, 0.109375, ((1, 2), (2, 16))),
        "norm_gains": jnp.clip(1.0 + 0.1 * jax.random.normal(splits[8], (LAYERS, 2, D), jnp.float32), 0.5, 1.5).astype(jnp.bfloat16),
        "shifts": noise(splits[9], (LAYERS, 4, D), 0.3, 2.0, ((2, 16),)),
        "cotangent": heavy_noise(splits[10], (MICRO, ROWS, LEN, D), 1.0, 6.0, ((1, 16), (2, 2)), (1, 3, 16, 2.0)),
    }


@jax.custom_vjp
def low(v):
    return lax.optimization_barrier(v.astype(jnp.bfloat16)).astype(jnp.float32)

@jax.custom_vjp
def low_back(v):
    return v

def low_keep(v):
    return (low(v), None)

def low_pass(kept, grad):
    return (grad,)

def back_keep(v):
    return (v, None)

def back_low(kept, grad):
    return (low(grad),)
low.defvjp(low_keep, low_pass)
low_back.defvjp(back_keep, back_low)

def layer_norm(summed, gain, shift):
    center = summed - lax.optimization_barrier(jnp.mean(summed, axis=-1, keepdims=True))
    spread = lax.optimization_barrier(jnp.mean(center * center, axis=-1, keepdims=True))
    return center * lax.rsqrt(spread + 1e-12) * gain + shift

def segment_ids(row_lengths):
    finish = jnp.cumsum(row_lengths, dtype=jnp.int32)
    places = jnp.arange(LEN, dtype=jnp.int32)
    return lax.optimization_barrier(jnp.sum((places[:, None] >= finish[None, :]).astype(jnp.int32), axis=1, dtype=jnp.int32))

def attend(packed):
    projected, segment = packed
    queries = projected[:, 0].reshape(LEN, H, HD)
    keys_all = projected[:, 1].reshape(LEN, H, HD)
    values_all = projected[:, 2].reshape(LEN, H, HD)
    raw_scores = jnp.einsum('qhd,khd->hqk', queries, keys_all, precision=lax.Precision.HIGHEST) * 0.125
    allowed = segment[:, None] == segment[None, :]
    scores = low_back(jnp.where(allowed[None], raw_scores, -1000000000.0))
    weights = low(jax.nn.softmax(scores, axis=-1))
    context = jnp.einsum('hqk,khd->qhd', weights, values_all, precision=lax.Precision.HIGHEST)
    return context.reshape(LEN, D)

def one_layer(hidden, segments, layer_weights):
    layer_qkv, layer_qkv_bias, layer_out, layer_up, layer_up_bias, layer_down, layer_gains, layer_shifts = layer_weights
    entering = low(hidden)
    projected = jnp.einsum('gtd,kdc->gtkc', entering, layer_qkv, precision=lax.Precision.HIGHEST)
    bias_rows = layer_qkv_bias.reshape(2, D)
    bias_all = jnp.stack([bias_rows[0], jnp.zeros((D,), jnp.float32), bias_rows[1]])
    projected = low_back(low(projected + bias_all))
    context = lax.map(jax.checkpoint(attend), (projected, segments))
    context = low_back(low(context))
    attended = jnp.einsum('gtc,cd->gtd', context, layer_out, precision=lax.Precision.HIGHEST)
    first_sum = hidden + low_back(attended) + layer_shifts[0]
    normed = layer_norm(first_sum, layer_gains[0], layer_shifts[1])
    widened = jnp.einsum('gtd,df->gtf', low(normed), layer_up, precision=lax.Precision.HIGHEST)
    widened = low_back(widened + layer_up_bias.reshape(FF))
    activated = low(jax.nn.gelu(widened, approximate=False))
    narrowed = jnp.einsum('gtf,fd->gtd', activated, layer_down, precision=lax.Precision.HIGHEST)
    second_sum = normed + low_back(narrowed) + layer_shifts[2]
    return layer_norm(second_sum, layer_gains[1], layer_shifts[3])

def reference(tokens, lengths, qkv_weight, qkv_bias, out_weight, up_weight, up_bias, down_weight, norm_gains, shifts, cotangent):
    weights_all = tuple((member.astype(jnp.float32) for member in (qkv_weight, qkv_bias, out_weight, up_weight, up_bias, down_weight, norm_gains, shifts)))
    group_rows = math.gcd(MICRO * ROWS, max(1, 4096 // LEN))
    groups = MICRO * ROWS // group_rows
    inputs = tokens.astype(jnp.float32).reshape(groups, group_rows, LEN, D)
    seeds = cotangent.astype(jnp.float32).reshape(groups, group_rows, LEN, D)
    segments = jax.vmap(segment_ids)(lengths.reshape(MICRO * ROWS, DOCS)).reshape(groups, group_rows, LEN)

    def forward(params, hidden, segment_rows):
        for layer_index in range(LAYERS):
            hidden = one_layer(hidden, segment_rows, tuple((member[layer_index] for member in params)))
        return hidden

    def accumulate(totals, packed):
        hidden, segment_rows, seed_rows = packed
        result, pull_back = jax.vjp(lambda params, initial: forward(params, initial, segment_rows), weights_all, hidden)
        weight_grads, input_grads = pull_back(seed_rows)
        return (jax.tree.map(jnp.add, totals, weight_grads), (result, input_grads))
    zero_grads = jax.tree.map(jnp.zeros_like, weights_all)
    totals, (results, input_grads) = lax.scan(accumulate, zero_grads, (inputs, segments, seeds))
    full_shape = (MICRO, ROWS, LEN, D)
    return (results.reshape(full_shape), input_grads.reshape(full_shape), totals[0], totals[1], totals[2], totals[3], totals[4], totals[5], totals[6], totals[7])
```

```python
import jax
import jax.numpy as jnp
from jax import lax
from jax.sharding import PartitionSpec as P

HD = 64
SQRT_HALF = 0.7071067811865476
DENSITY_SCALE = 0.3989422804014327
F32 = jnp.float32
BF16 = jnp.bfloat16
SMALL = 128


def dp_coords():
    index = lax.axis_index("dp")
    return index // 4, (index // 2) % 2, index % 2


def swap(value, bit):
    return lax.ppermute(value, "dp", [(i, i ^ bit) for i in range(16)])


def z_move(value, step, lines):
    return lax.ppermute(
        value, "dp", [(4 * i + j, 4 * (i + step) + j) for i in lines for j in range(4)]
    )


def other_core(value):
    return lax.ppermute(value, "tensor", [(0, 1), (1, 0)])


def ordered(bit, mine, theirs):
    return jnp.stack([jnp.where(bit == 0, mine, theirs), jnp.where(bit == 0, theirs, mine)])


def z_gather(own, z):
    right, left = [own], [own]
    for k in range(3):
        right.append(z_move(right[-1], 1, range(k, 3)))
        left.append(z_move(left[-1], -1, range(3 - k, 0, -1)))
    around = [own] + [jnp.where(z >= k, right[k], left[4 - k]) for k in (1, 2, 3)]
    placed = []
    for source in range(4):
        chosen = around[0]
        for k in (1, 2, 3):
            chosen = jnp.where((z - source) % 4 == k, around[k], chosen)
        placed.append(chosen)
    return jnp.stack(placed)


def gather_grid(shard):
    z, y, x = dp_coords()
    rows = shard.shape[0] // 3
    first, rest = shard[:rows], shard[rows:]
    a_x = ordered(x, first, swap(first, 1))
    a_yx = ordered(y, a_x, swap(a_x, 2))
    lines = z_gather(rest, z)
    a = z_gather(a_yx, z)
    b, c = lines[:, :rows], lines[:, rows:]
    b_x = ordered(x, b, swap(b, 1))
    b_yx = ordered(y, b_x, swap(b_x, 2))
    c_y = ordered(y, c, swap(c, 2))
    c_xy = ordered(x, c_y, swap(c_y, 1))
    whole = jnp.stack([a, b_yx.transpose(2, 0, 1, 3, 4), c_xy.transpose(2, 1, 0, 3, 4)], axis=3)
    return whole.reshape(16 * shard.shape[0], shard.shape[1])


def z_reduce(parts, z):
    def chunk(k):
        return lax.dynamic_index_in_dim(parts, jnp.clip(k, 0, 3), 0, keepdims=False)

    r_in = l_in = None
    for s in (1, 2, 3):
        send_r, send_l = chunk(z + 4 - s), chunk(z - 4 + s)
        if s > 1:
            send_r = (send_r.astype(F32) + jnp.where(z > 0, r_in.astype(F32), 0.0)).astype(BF16)
            send_l = (send_l.astype(F32) + jnp.where(z < 3, l_in.astype(F32), 0.0)).astype(BF16)
        r_in = z_move(send_r, 1, range(0, s))
        l_in = z_move(send_l, -1, range(3, 3 - s, -1))
    return chunk(z).astype(F32) + r_in.astype(F32) + l_in.astype(F32)


def swap_reduce(parts, bit, place, dim):
    theirs = lax.dynamic_index_in_dim(parts, 1 - place, dim, keepdims=False).astype(BF16)
    mine = lax.dynamic_index_in_dim(parts, place, dim, keepdims=False).astype(F32)
    return mine + swap(theirs, bit).astype(F32)


def reduce_grid(partial):
    z, y, x = dp_coords()
    rows, columns = partial.shape[0] // 48, partial.shape[1]
    grid = partial.reshape(4, 2, 2, 3, rows, columns)
    a, b, c = grid[:, :, :, 0], grid[:, :, :, 1], grid[:, :, :, 2]
    b = swap_reduce(swap_reduce(b, 2, y, 1), 1, x, 1).astype(BF16)
    c = swap_reduce(swap_reduce(c, 1, x, 2), 2, y, 1).astype(BF16)
    a = z_reduce(a, z)
    rest = z_reduce(jnp.concatenate([b, c], 1), z)
    a = swap_reduce(swap_reduce(a, 1, x, 1), 2, y, 0)
    return jnp.concatenate([a, rest], 0)


def gather_dp(shard):
    if lax.axis_size("dp") == 16:
        return gather_grid(shard)
    return lax.all_gather(shard, "dp", axis=0, tiled=True)


def reduce_dp(partial):
    if lax.axis_size("dp") == 16:
        return reduce_grid(partial)
    return lax.psum_scatter(partial.astype(F32), "dp", scatter_dimension=0, tiled=True)


def segment_ids(row_lengths, length):
    finish = jnp.cumsum(row_lengths, dtype=jnp.int32)
    places = jnp.arange(length, dtype=jnp.int32)
    return jnp.sum((places[:, None] >= finish[None, :]).astype(jnp.int32), axis=1, dtype=jnp.int32)


def norm_forward(summed, gain, shift):
    center = summed - jnp.mean(summed, axis=-1, keepdims=True)
    spread = jnp.mean(center * center, axis=-1, keepdims=True)
    scaling = lax.rsqrt(spread + 1e-12)
    normal = center * scaling
    return (normal * gain + shift, normal, scaling)


def norm_backward(upstream, normal, scaling, gain):
    gain_part = jnp.sum(upstream * normal, axis=0)
    shift_part = jnp.sum(upstream, axis=0)
    scaled = upstream * gain
    centered = scaled - jnp.mean(scaled, axis=-1, keepdims=True)
    back = scaling * (centered - normal * jnp.mean(scaled * normal, axis=-1, keepdims=True))
    return (back, gain_part, shift_part)


def nn(a, b):
    return jnp.dot(a, b, preferred_element_type=F32)


def nt(a, b):
    return lax.dot_general(a, b, (((1,), (1,)), ((), ())), preferred_element_type=F32)


def tn(a, b):
    return lax.dot_general(a, b, (((0,), (0,)), ((), ())), preferred_element_type=F32)


def heads_of(part, heads):
    return part.reshape(part.shape[0], heads, HD).transpose(1, 0, 2)


def attention(q, k, v, allowed):
    heads = q.shape[1] // HD
    q, k, v = (heads_of(t, heads) for t in (q, k, v))
    scores = jnp.einsum("hqd,hkd->hqk", q, k, preferred_element_type=F32) * 0.125
    scores = jnp.where(allowed[None], scores, -1000000000.0)
    highest = jnp.max(scores, axis=-1, keepdims=True)
    raised = jnp.exp(scores - highest)
    total = jnp.sum(raised, axis=-1, keepdims=True)
    weights = (raised / total).astype(BF16)
    context = jnp.einsum("hqk,hkd->hqd", weights, v, preferred_element_type=F32).astype(BF16)
    return context.transpose(1, 0, 2).reshape(q.shape[1], heads * HD), highest + jnp.log(total)


def attention_back(q, k, v, allowed, log_totals, context_grad):
    heads = q.shape[1] // HD
    length = q.shape[0]
    q, k, v, g = (heads_of(t, heads) for t in (q, k, v, context_grad))
    scores = jnp.einsum("hqd,hkd->hqk", q, k, preferred_element_type=F32) * 0.125
    scores = jnp.where(allowed[None], scores, -1000000000.0)
    weights = jnp.exp(scores - log_totals)
    dv = jnp.einsum("hqk,hqd->hkd", weights.astype(BF16), g, preferred_element_type=F32)
    dw = jnp.einsum("hqd,hkd->hqk", g, v, preferred_element_type=F32)
    inner = jnp.sum(weights * dw, axis=-1, keepdims=True)
    ds = (weights * (dw - inner)).astype(BF16)
    dq = jnp.einsum("hqk,hkd->hqd", ds, k, preferred_element_type=F32) * 0.125
    dk = jnp.einsum("hqk,hqd->hkd", ds, q, preferred_element_type=F32) * 0.125
    return [t.astype(BF16).transpose(1, 0, 2).reshape(length, heads * HD) for t in (dq, dk, dv)]


class Sizes:
    def __init__(self, qkv, out, up):
        self.part = qkv.shape[3]
        self.hidden = up.shape[2]
        p = self.part
        self.qkv = slice(0, 3 * p)
        self.out = slice(3 * p, 4 * p)
        self.up = slice(4 * p, 4 * p + self.hidden)
        self.down = slice(4 * p + self.hidden, 4 * p + 2 * self.hidden)
        self.small = slice(4 * p + 2 * self.hidden, 4 * p + 2 * self.hidden + SMALL)


def pack(qkv, qkv_bias, out, up, up_bias, down, gains, shifts):
    rows = qkv.shape[1]
    small = jnp.concatenate(
        [
            gains.T,
            shifts.T,
            qkv_bias.reshape(rows, -1),
            up_bias.reshape(-1, rows).T,
        ],
        axis=1,
    )
    small = jnp.pad(small, ((0, 0), (0, SMALL - small.shape[1])))
    return jnp.concatenate(
        [qkv.transpose(1, 0, 2).reshape(rows, -1), out.T, up, down.T, small], axis=1
    )


def unpack_small(small, rows):
    shards = small.shape[0] // rows
    values = small.astype(F32)
    gains, shifts = values[:, :2].T, values[:, 2:6].T
    qkv_bias = values[:, 6].reshape(shards, 2, rows // 2).transpose(1, 0, 2).reshape(2, -1)
    up_bias = values[:, 7:9].reshape(shards, rows, 2).transpose(0, 2, 1).reshape(-1)
    return gains, shifts, qkv_bias, up_bias


def pack_small_grads(gains, shifts, qkv_bias, up_bias, rows):
    shards = gains.shape[1] // rows
    columns = [
        gains.T,
        shifts.T,
        qkv_bias.reshape(2, shards, rows // 2).transpose(1, 0, 2).reshape(-1, 1),
        up_bias.reshape(shards, 2, rows).transpose(0, 2, 1).reshape(-1, 2),
    ]
    small = jnp.concatenate(columns, axis=1)
    return jnp.pad(small, ((0, 0), (0, SMALL - small.shape[1])))


def forward_layer(x, allowed, mine, theirs, smalls, sizes):
    gains, shifts, qb_m, ub_m, qb_t, ub_t = smalls
    p = sizes.part
    entering = x.astype(BF16)
    zero = jnp.zeros((p,), F32)

    def project(weights, qb):
        bias = jnp.concatenate([qb[0], zero, qb[1]])
        return (nn(entering, weights[:, sizes.qkv]) + bias).astype(BF16)

    proj_m, proj_t = project(mine, qb_m), project(theirs, qb_t)
    ctx_m, log_m = attention(proj_m[:, :p], proj_m[:, p : 2 * p], proj_m[:, 2 * p :], allowed)
    ctx_t, log_t = attention(proj_t[:, :p], proj_t[:, p : 2 * p], proj_t[:, 2 * p :], allowed)
    first_sum = x + nt(ctx_m, mine[:, sizes.out]) + nt(ctx_t, theirs[:, sizes.out]) + shifts[0]
    normed, normal_one, scale_one = norm_forward(first_sum, gains[0], shifts[1])
    widened_in = normed.astype(BF16)
    wide_m = nn(widened_in, mine[:, sizes.up]) + ub_m
    wide_t = nn(widened_in, theirs[:, sizes.up]) + ub_t

    def gelu(w):
        return (0.5 * w * (1.0 + lax.erf(w * SQRT_HALF))).astype(BF16)

    act_m, act_t = gelu(wide_m), gelu(wide_t)
    second_sum = (
        normed + nt(act_m, mine[:, sizes.down]) + nt(act_t, theirs[:, sizes.down]) + shifts[2]
    )
    result, normal_two, scale_two = norm_forward(second_sum, gains[1], shifts[3])
    both = dict(
        entering=jnp.concatenate([entering, other_core(entering)]),
        ctx=jnp.concatenate([ctx_m, other_core(ctx_t)]),
        widened_in=jnp.concatenate([widened_in, other_core(widened_in)]),
        act=jnp.concatenate([act_m, other_core(act_t)]),
    )
    stored = (
        proj_m,
        proj_t,
        log_m,
        log_t,
        normal_one,
        scale_one,
        wide_m,
        wide_t,
        normal_two,
        scale_two,
        both,
    )
    return result, stored


def backward_layer(upstream, allowed, mine, theirs, smalls, stored, sizes):
    gains = smalls[0]
    proj_m, proj_t, log_m, log_t, normal_one, scale_one, wide_m, wide_t, normal_two, scale_two, both = stored
    p = sizes.part
    second_grad, gain_two, shift_two = norm_backward(upstream, normal_two, scale_two, gains[1])
    down_seed = second_grad.astype(BF16)

    def slope(w):
        return (
            0.5 * (1.0 + lax.erf(w * SQRT_HALF)) + w * jnp.exp(-0.5 * w * w) * DENSITY_SCALE
        )

    wg_m = (nn(down_seed, mine[:, sizes.down]) * slope(wide_m)).astype(BF16)
    wg_t = (nn(down_seed, theirs[:, sizes.down]) * slope(wide_t)).astype(BF16)
    seeds = jnp.concatenate([down_seed, other_core(down_seed)])
    down_grad = tn(seeds, both["act"])
    wg_both = jnp.concatenate([wg_m, other_core(wg_t)])
    up_grad = tn(both["widened_in"], wg_both)
    up_bias_grad = jnp.sum(wg_both.astype(F32), axis=0)
    normed_grad = second_grad + nt(wg_m, mine[:, sizes.up]) + nt(wg_t, theirs[:, sizes.up])
    first_grad, gain_one, shift_one = norm_backward(normed_grad, normal_one, scale_one, gains[0])
    out_seed = first_grad.astype(BF16)
    seeds = jnp.concatenate([out_seed, other_core(out_seed)])
    out_grad = tn(seeds, both["ctx"])
    cg_m = nn(out_seed, mine[:, sizes.out]).astype(BF16)
    cg_t = nn(out_seed, theirs[:, sizes.out]).astype(BF16)
    pg_m = attention_back(
        proj_m[:, :p], proj_m[:, p : 2 * p], proj_m[:, 2 * p :], allowed, log_m, cg_m
    )
    pg_t = attention_back(
        proj_t[:, :p], proj_t[:, p : 2 * p], proj_t[:, 2 * p :], allowed, log_t, cg_t
    )
    pg_m, pg_t = jnp.concatenate(pg_m, axis=1), jnp.concatenate(pg_t, axis=1)
    pg_both = jnp.concatenate([pg_m, other_core(pg_t)])
    qkv_grad = tn(both["entering"], pg_both)
    column_sums = jnp.sum(pg_both.astype(F32), axis=0)
    qkv_bias_grad = jnp.stack([column_sums[:p], column_sums[2 * p :]])
    input_grad = first_grad + nt(pg_m, mine[:, sizes.qkv]) + nt(pg_t, theirs[:, sizes.qkv])
    norms = jnp.stack(
        [gain_one, gain_two, jnp.sum(first_grad, axis=0), shift_one, jnp.sum(second_grad, axis=0), shift_two]
    )
    norms = norms + other_core(norms)
    return input_grad, (qkv_grad, out_grad, up_grad, down_grad, norms, qkv_bias_grad, up_bias_grad)


def on_device(
    tokens,
    lengths,
    qkv_weight,
    qkv_bias,
    out_weight,
    up_weight,
    up_bias,
    down_weight,
    norm_gains,
    shifts,
    cotangent,
):
    layers = qkv_weight.shape[0]
    micro, half = tokens.shape[0], tokens.shape[2]
    assert micro == 2 and lax.axis_size("tensor") == 2 and tokens.shape[1] == 1
    length = 2 * half
    core = lax.axis_index("tensor")
    sizes = Sizes(qkv_weight, out_weight, up_weight)
    rows = qkv_weight.shape[2]

    def whole_row(values):
        kept = lax.dynamic_index_in_dim(values[:, 0], core, 0, keepdims=False)
        given = lax.dynamic_index_in_dim(values[:, 0], 1 - core, 0, keepdims=False)
        return jnp.concatenate([kept, other_core(given)], axis=0).astype(F32)

    def split_row(row):
        kept, given = row[:half], row[half:]
        back = other_core(given)
        return jnp.stack([jnp.where(core == 0, kept, back), jnp.where(core == 0, back, kept)])[:, None]

    segment = segment_ids(lax.dynamic_index_in_dim(lengths[:, 0], core, 0, keepdims=False), length)
    segment = jnp.where(core == 0, segment, jnp.roll(segment, half))
    allowed = segment[:, None] == segment[None, :]

    weights, smalls = [], []
    params = (qkv_weight, qkv_bias, out_weight, up_weight, up_bias, down_weight, norm_gains, shifts)
    for layer in range(layers):
        shard = pack(*(member[layer] for member in params))
        mine = gather_dp(shard)
        theirs = other_core(mine)
        gains, shift_rows, qb_m, ub_m = unpack_small(mine[:, sizes.small], rows)
        _, _, qb_t, ub_t = unpack_small(theirs[:, sizes.small], rows)
        weights.append((mine, theirs))
        smalls.append((gains, shift_rows, qb_m, ub_m, qb_t, ub_t))

    hidden = whole_row(tokens)
    stored = []
    for layer in range(layers):
        hidden, kept = forward_layer(hidden, allowed, *weights[layer], smalls[layer], sizes)
        stored.append(kept)
    out_tokens = split_row(hidden)
    upstream = whole_row(cotangent)
    grads = [None] * layers
    for layer in reversed(range(layers)):
        upstream, found = backward_layer(
            upstream, allowed, *weights[layer], smalls[layer], stored[layer], sizes
        )
        qkv_grad, out_grad, up_grad, down_grad, norms, qkv_bias_grad, up_bias_grad = found
        small = pack_small_grads(norms[:2], norms[2:], qkv_bias_grad, up_bias_grad, rows)
        partial = jnp.concatenate([qkv_grad, out_grad, up_grad, down_grad, small], axis=1).astype(BF16)
        total = reduce_dp(partial)
        small = total[:, sizes.small]
        grads[layer] = (
            total[:, sizes.qkv].reshape(rows, 3, -1).transpose(1, 0, 2),
            small[:, 6].reshape(2, 1, -1),
            total[:, sizes.out].T,
            total[:, sizes.up],
            small[:, 7:9].T.reshape(1, -1),
            total[:, sizes.down].T,
            small[:, :2].T,
            small[:, 2:6].T,
        )
    token_grad = split_row(upstream)
    stacked = [jnp.stack([grads[layer][i] for layer in range(layers)]) for i in range(8)]
    return (out_tokens, token_grad, *stacked)


def solution(mesh):
    in_specs = (
        P(None, "dp", "tensor", None),
        P(None, "dp", None),
        P(None, None, "dp", "tensor"),
        P(None, None, "tensor", "dp"),
        P(None, "tensor", "dp"),
        P(None, "dp", "tensor"),
        P(None, "tensor", "dp"),
        P(None, "tensor", "dp"),
        P(None, None, "dp"),
        P(None, None, "dp"),
        P(None, "dp", "tensor", None),
    )
    out_specs = (
        P(None, "dp", "tensor", None),
        P(None, "dp", "tensor", None),
        P(None, None, "dp", "tensor"),
        P(None, None, "tensor", "dp"),
        P(None, "tensor", "dp"),
        P(None, "dp", "tensor"),
        P(None, "tensor", "dp"),
        P(None, "tensor", "dp"),
        P(None, None, "dp"),
        P(None, None, "dp"),
    )
    return jax.shard_map(
        on_device, mesh=mesh, in_specs=in_specs, out_specs=out_specs, check_vma=False
    )
```
